32 devices in a mesh: dp: 8 (over z, x), ctx: 4 (over y, core).
Axes of the slice: x: 2, y: 2, z: 4, core: 2. Of those that a mesh axis runs over, the one named last changes fastest.
Arguments:
- inputs: bfloat16 [8, 512, 5376], P('dp', 'ctx'), may hold values from -6 to 6
- q_proj: bfloat16 [8, 512, 2048], P('dp', 'ctx'), may hold values from -260 to 260
- k_proj: bfloat16 [8, 512, 1024], P('dp', 'ctx'), may hold values from -260 to 260
- v_proj: bfloat16 [8, 512, 1024], P('dp', 'ctx'), may hold values from -6 to 6
- d_attn: bfloat16 [8, 512, 2048], P('dp', 'ctx'), may hold values from -6 to 6
- positions: int32 [8, 512], P('dp', 'ctx'), may hold values from 0 to 511, as said below
- windows: int32 [8], P('dp'), may hold values from 512 to 1024
- q_gain: float32 [128], replicated, may hold values from 0.7 to 5.5
- k_gain: float32 [128], replicated, may hold values from 0.7 to 5.5
- weight: bfloat16 [5376, 4096], P('dp'), may hold values from -0.078125 to 0.078125
Outputs:
- d_inputs: bfloat16 [8, 512, 5376], P('dp', 'ctx')
- d_weight_t: float32 [4096, 5376], P('ctx', 'dp')
- d_q_gain: float32 [128], replicated
- d_k_gain: float32 [128], replicated
The draws below stay inside these ranges and needn't reach their ends.
Inputs may be any that keep to these rules, and one draw needn't show every extreme that they name: `positions`: within each sequence a position counts the tokens since its document began: it grows by one from token to token and falls to 0 where a document begins; the first token of a sequence has position 0. Some sequence holds a single document.
All inputs are finite; a program needn't handle non-finite values.
Results may differ from the reference program's by a relative error of at most 0.029.
Values may be sent and summed in bfloat16 or wider, within the bound.
A program may use at most 128 MiB of HBM per device.

```python
import math
import jax
import jax.numpy as jnp
from jax import lax

D = 5376
QUERY_HEADS = 16
KEY_HEADS = 8
HEAD_SIZE = 128
WIN = 1024
TOK_DEV = 128
QUERY_GROUP = 2
QW = 2048
KW = 1024
PW = 4096
REACH = 8
SEQUENCE_LENGTH = 512
BATCH_COUNT = 8
N_CTX = 4


def draw_heads(key):
    flow_count = jax.random.split(jax.random.fold_in(key, 7), 5)
    column_scale = jnp.exp(jax.random.uniform(flow_count[0], (HEAD_SIZE,), jnp.float32, math.log(0.4), math.log(4.0)))
    query_scale = jnp.exp(jax.random.uniform(flow_count[1], (BATCH_COUNT, SEQUENCE_LENGTH, QUERY_HEADS, 1), jnp.float32, math.log(0.5), math.log(5.0)))
    key_norm_scale = jnp.exp(jax.random.uniform(flow_count[2], (BATCH_COUNT, SEQUENCE_LENGTH, KEY_HEADS, 1), jnp.float32, math.log(0.5), math.log(5.0)))
    query_rows = jax.random.truncated_normal(flow_count[3], -6.0, 6.0, (BATCH_COUNT, SEQUENCE_LENGTH, QUERY_HEADS, HEAD_SIZE), jnp.float32)
    key_unnormed = jax.random.truncated_normal(flow_count[4], -6.0, 6.0, (BATCH_COUNT, SEQUENCE_LENGTH, KEY_HEADS, HEAD_SIZE), jnp.float32)
    return (query_rows * query_scale * column_scale, key_unnormed * key_norm_scale * column_scale)


def draw_q_proj(key, part):
    query_rows, key_output = draw_heads(key)
    return query_rows.reshape(BATCH_COUNT, SEQUENCE_LENGTH, QUERY_HEADS * HEAD_SIZE).astype(jnp.bfloat16)


def draw_k_proj(key, part):
    query_rows, key_output = draw_heads(key)
    return key_output.reshape(BATCH_COUNT, SEQUENCE_LENGTH, KEY_HEADS * HEAD_SIZE).astype(jnp.bfloat16)


def draw_positions(key, part):
    marks = jax.random.randint(jax.random.fold_in(key, 3), (BATCH_COUNT, 2), 1, 3 * SEQUENCE_LENGTH)
    single = jax.random.randint(jax.random.fold_in(key, 5), (), 0, BATCH_COUNT)
    marks = jnp.where((jnp.arange(BATCH_COUNT) == single)[:, None], SEQUENCE_LENGTH, marks)
    index = jnp.arange(SEQUENCE_LENGTH, dtype=jnp.int32)[None, :, None]
    begun = jnp.where(marks[:, None, :] <= index, marks[:, None, :], 0)
    return (index[:, :, 0] - jnp.max(begun, axis=-1)).astype(jnp.int32)


def draw_windows(key, part):
    flow_count = jax.random.split(jax.random.fold_in(key, 4), 3)
    drawn = jax.random.randint(flow_count[0], (BATCH_COUNT,), WIN // 2, WIN + 1)
    widest = jax.random.randint(flow_count[1], (), 0, BATCH_COUNT)
    narrowest = (widest + 1 + jax.random.randint(flow_count[2], (), 0, BATCH_COUNT - 1)) % BATCH_COUNT
    slots = jnp.arange(BATCH_COUNT)
    result = jnp.where(slots == widest, WIN, jnp.where(slots == narrowest, WIN // 2, drawn))
    return result.astype(jnp.int32)


def draw_q_gain(key, part):
    return jax.random.uniform(jax.random.fold_in(key, 11), (HEAD_SIZE,), jnp.float32, 0.7, 1.3)


def draw_k_gain(key, part):
    return jax.random.uniform(jax.random.fold_in(key, 12), (HEAD_SIZE,), jnp.float32, 0.7, 1.3)


def strengthened(values, rng, source, target, blocks, factor):
    owner, partner = [(jnp.arange(values.shape[position]) // (values.shape[position] // blocks)).reshape([-1 if axis == position else 1 for axis in range(values.ndim)]) for position in (source, target)]
    chosen = jax.random.permutation(rng, blocks)[partner]
    strong = (owner == chosen) | (owner == (partner + blocks // 2) % blocks)
    return jnp.where(strong, factor * values, values)


def levels(key, extent, pieces, low, high):
    loudness = 1.0
    for axis_at, parts in pieces:
        draws = jax.random.uniform(jax.random.fold_in(jax.random.fold_in(key, 6), axis_at), (parts,), jnp.float32, low / len(pieces), high / len(pieces))
        loudness = loudness * jnp.repeat(jnp.exp(draws), extent[axis_at] // parts).reshape((-1,) + (1,) * (len(extent) - 1 - axis_at))
    return loudness


def centred(rng, dims, spread, reach, cuts=(), kind=jnp.bfloat16):
    values = jax.random.normal(rng, dims, jnp.float32) * spread
    if len(cuts) > 0:
        values = levels(rng, dims, cuts, -0.22, 0.18) * values
    return jnp.clip(values, min=-reach, max=reach).astype(kind)


def bell_draw_with(key, extent, scale, bound, pieces, heavy, kind=jnp.bfloat16):
    entries = scale * jax.random.normal(key, extent, jnp.float32)
    if pieces:
        entries = entries * levels(key, extent, pieces, -0.22, 0.18)
    return jnp.clip(strengthened(entries, jax.random.fold_in(key, 3), *heavy), -bound, bound).astype(kind)


def setup_inputs(seed: int = 0) -> dict:
    seeds = jax.random.split(jax.random.key(seed), 11)
    return {
        "inputs": centred(seeds[0], (BATCH_COUNT, SEQUENCE_LENGTH, D), 1.0, 6.0, ((0, 8), (1, 4))),
        "q_proj": draw_q_proj(jax.random.fold_in(seeds[10], 71), 0),
        "k_proj": draw_k_proj(jax.random.fold_in(seeds[10], 71), 0),
        "v_proj": centred(seeds[3], (BATCH_COUNT, SEQUENCE_LENGTH, KW), 1.0, 6.0, ((0, 8), (1, 4))),
        "d_attn": bell_draw_with(seeds[4], (BATCH_COUNT, SEQUENCE_LENGTH, QW), 0.5, 6.0, ((0, 8), (1, 4)), (1, 2, 4, 2.0)),
        "positions": draw_positions(jax.random.fold_in(seeds[10], 71), 0),
        "windows": draw_windows(jax.random.fold_in(seeds[10], 71), 0),
        "q_gain": draw_q_gain(jax.random.fold_in(seeds[10], 71), 0),
        "k_gain": draw_k_gain(jax.random.fold_in(seeds[10], 71), 0),
        "weight": centred(seeds[9], (D, PW), D ** -0.5, 0.078125, ((0, 8),)),
    }


score_scale = 168.0 ** (-0.5)
rope_base = 10000.0
norm_eps = 1e-06

def rotated_unit(projected_rows, gain_vector, token_pos, head_count):
    head_width = gain_vector.shape[0]
    rows_heads = projected_rows.reshape(projected_rows.shape[0], head_count, head_width)
    inverse = lax.rsqrt(lax.optimization_barrier(jnp.mean(rows_heads * rows_heads, axis=-1, keepdims=True)) + norm_eps)
    normed = rows_heads * inverse * gain_vector
    half_width = head_width // 2
    frequency = jnp.exp(jnp.arange(half_width, dtype=jnp.float32) * (-2.0 * math.log(rope_base) / head_width))
    angles = token_pos.astype(jnp.float32)[:, None] * frequency[None, :]
    cosine_table = jnp.cos(angles)[:, None, :]
    sine_table = jnp.sin(angles)[:, None, :]
    first_half = normed[..., :half_width]
    second_half = normed[..., half_width:]
    return jnp.concatenate([first_half * cosine_table - second_half * sine_table, second_half * cosine_table + first_half * sine_table], axis=-1)

def rounded_outside(values, keep_mask):
    low = lax.optimization_barrier(values.astype(jnp.bfloat16)).astype(jnp.float32)
    return jnp.where(keep_mask, values, low)

def sequence_grads(q_seq, k_seq, value_sequence, sequence_gradient, position_sequence, window, q_gain, k_gain):

    def query_side(projected_rows, gain_vector):
        return rotated_unit(projected_rows, gain_vector, position_sequence, QUERY_HEADS)

    def key_side(projected_rows, gain_vector):
        return rotated_unit(projected_rows, gain_vector, position_sequence, KEY_HEADS)
    q_full, query_back = jax.vjp(query_side, q_seq.astype(jnp.float32), q_gain)
    k_full, key_back = jax.vjp(key_side, k_seq.astype(jnp.float32), k_gain)
    query_rotated = q_full.astype(jnp.bfloat16)
    key_rotated = k_full.astype(jnp.bfloat16)
    value_heads = value_sequence.reshape(SEQUENCE_LENGTH, KEY_HEADS, HEAD_SIZE)
    head_gradient = sequence_gradient.reshape(SEQUENCE_LENGTH, KEY_HEADS, QUERY_GROUP, HEAD_SIZE)
    query_grouped = query_rotated.reshape(SEQUENCE_LENGTH, KEY_HEADS, QUERY_GROUP, HEAD_SIZE)
    pad_amount = REACH * TOK_DEV
    span_rows = (REACH + 1) * TOK_DEV
    key_padded = jnp.concatenate([jnp.zeros((pad_amount, KEY_HEADS, HEAD_SIZE), jnp.bfloat16), key_rotated], axis=0)
    value_padded = jnp.concatenate([jnp.zeros((pad_amount, KEY_HEADS, HEAD_SIZE), jnp.bfloat16), value_heads], axis=0)
    query_off = jnp.arange(TOK_DEV, dtype=jnp.int32)
    key_off = jnp.arange(span_rows, dtype=jnp.int32)
    own_rows = (key_off >= pad_amount)[:, None, None]

    def block_step(carry, index):
        dk_acc, dv_acc = carry
        start_row = (index * TOK_DEV).astype(jnp.int32)
        q_block = lax.dynamic_slice_in_dim(query_grouped, start_row, TOK_DEV, 0).astype(jnp.float32)
        d_block = lax.dynamic_slice_in_dim(head_gradient, start_row, TOK_DEV, 0).astype(jnp.float32)
        pos_block = lax.dynamic_slice_in_dim(position_sequence, start_row, TOK_DEV, 0)
        k_window = lax.dynamic_slice_in_dim(key_padded, start_row, span_rows, 0).astype(jnp.float32)
        v_window = lax.dynamic_slice_in_dim(value_padded, start_row, span_rows, 0).astype(jnp.float32)
        distance = query_off[:, None] + pad_amount - key_off[None, :]
        allowed = (distance >= 0) & (distance < window) & (distance <= pos_block[:, None])
        scores = jnp.einsum('ahgd,chd->hgac', q_block, k_window) * score_scale
        scores = jnp.where(allowed, scores, -jnp.inf)
        row_max = lax.optimization_barrier(jnp.max(scores, axis=-1, keepdims=True))
        exponent = jnp.exp(scores - row_max)
        probs = exponent / lax.optimization_barrier(jnp.sum(exponent, axis=-1, keepdims=True))
        dprobs = jnp.einsum('ahgd,chd->hgac', d_block, v_window)
        delta = lax.optimization_barrier(jnp.sum(probs * dprobs, axis=-1, keepdims=True))
        dscores = (probs * (dprobs - delta)).astype(jnp.bfloat16).astype(jnp.float32)
        probs_low = probs.astype(jnp.bfloat16).astype(jnp.float32)
        dq_block = jnp.einsum('hgac,chd->ahgd', dscores, k_window) * score_scale
        dk_window = jnp.einsum('hgac,ahgd->chd', dscores, q_block) * score_scale
        dv_window = jnp.einsum('hgac,ahgd->chd', probs_low, d_block)
        dk_window = rounded_outside(dk_window, own_rows)
        dv_window = rounded_outside(dv_window, own_rows)
        dk_acc = lax.dynamic_update_slice_in_dim(dk_acc, lax.dynamic_slice_in_dim(dk_acc, start_row, span_rows, 0) + dk_window, start_row, 0)
        dv_acc = lax.dynamic_update_slice_in_dim(dv_acc, lax.dynamic_slice_in_dim(dv_acc, start_row, span_rows, 0) + dv_window, start_row, 0)
        return ((dk_acc, dv_acc), dq_block.reshape(TOK_DEV, QUERY_HEADS, HEAD_SIZE))
    blank_block = jnp.zeros((pad_amount + SEQUENCE_LENGTH, KEY_HEADS, HEAD_SIZE), jnp.float32)
    (dk_acc, dv_acc), dq_blocks = lax.scan(block_step, (blank_block, blank_block), jnp.arange(N_CTX, dtype=jnp.int32))
    dq_rot = dq_blocks.reshape(SEQUENCE_LENGTH, QUERY_HEADS, HEAD_SIZE)
    dk_rot = dk_acc[pad_amount:]
    dv_proj = dv_acc[pad_amount:].reshape(SEQUENCE_LENGTH, KW)
    dq_proj, dq_gain = query_back(dq_rot)
    dk_proj, dk_gain = key_back(dk_rot)
    d_proj = jnp.concatenate([dq_proj, dk_proj, dv_proj], axis=-1).astype(jnp.bfloat16)
    return (d_proj, dq_gain, dk_gain)

def reference(inputs, q_proj, k_proj, v_proj, d_attn, positions, windows, q_gain, k_gain, weight):

    def one_sequence(members):
        q_seq, k_seq, value_sequence, sequence_gradient, position_sequence, window = members
        return sequence_grads(q_seq, k_seq, value_sequence, sequence_gradient, position_sequence, window, q_gain, k_gain)
    d_proj, dq_gain, dk_gain = lax.map(one_sequence, (q_proj, k_proj, v_proj, d_attn, positions, windows))

    def input_grad(rows_seq):
        return jnp.dot(rows_seq, weight.T, preferred_element_type=jnp.float32).astype(jnp.bfloat16)
    d_inputs = lax.map(input_grad, d_proj)

    def weight_block(total, index):
        start_row = (index * TOK_DEV).astype(jnp.int32)
        grads_rows = lax.dynamic_slice_in_dim(d_proj, start_row, TOK_DEV, 1).reshape(BATCH_COUNT * TOK_DEV, PW)
        input_rows = lax.dynamic_slice_in_dim(inputs, start_row, TOK_DEV, 1).reshape(BATCH_COUNT * TOK_DEV, D)
        term = jnp.dot(grads_rows.T, input_rows, preferred_element_type=jnp.float32)
        return (total + lax.optimization_barrier(term.astype(jnp.bfloat16)).astype(jnp.float32), None)
    d_weight_t, _ = lax.scan(weight_block, jnp.zeros((PW, D), jnp.float32), jnp.arange(N_CTX, dtype=jnp.int32))
    return (d_inputs, d_weight_t, lax.optimization_barrier(jnp.sum(dq_gain, axis=0)), lax.optimization_barrier(jnp.sum(dk_gain, axis=0)))
```

```python
import math

import jax
import jax.numpy as jnp
from jax import lax
from jax.sharding import PartitionSpec as P

REACH = 8


score_scale = 168.0 ** (-0.5)
rope_base = 10000.0
norm_eps = 1e-06


def from_behind(value, axis, steps):
    count = lax.axis_size(axis)
    initial, last = (max(0, -steps), min(count, count - steps))
    return lax.ppermute(value, axis, [(source, source + steps) for source in range(initial, last)])


def swapped(value, axis, bit):
    count = lax.axis_size(axis)
    return lax.ppermute(value, axis, [(source, source ^ bit) for source in range(count)])


def halved(term, axis):
    owners = lax.axis_size(axis) // 2
    side = (lax.axis_index(axis) & 1) == 1
    pieces = term.reshape(owners // 2, 2, term.shape[0] // owners, term.shape[1])
    kept = jnp.where(side, pieces[:, 1], pieces[:, 0])
    sent = jnp.where(side, pieces[:, 0], pieces[:, 1])
    got = swapped(sent, axis, 1)
    return kept.astype(jnp.float32) + got.astype(jnp.float32)


def owner_sum(halves, axis):
    count = lax.axis_size(axis)
    index = lax.axis_index(axis)
    low, high = halves
    bit = count // 2
    while bit >= 2:
        side = (index & bit) != 0
        kept = jnp.where(side, high, low)
        sent = jnp.where(side, low, high).astype(jnp.bfloat16)
        total = kept + swapped(sent, axis, bit).astype(jnp.float32)
        middle = total.shape[0] // 2
        low, high = total[:middle], total[middle:]
        bit //= 2
    return total.reshape(-1, total.shape[-1])


def rotated_unit(projected_rows, gain_vector, token_pos, head_count):
    head_width = gain_vector.shape[0]
    rows_heads = projected_rows.reshape(projected_rows.shape[0], head_count, head_width)
    inverse = lax.rsqrt(jnp.mean(rows_heads * rows_heads, axis=-1, keepdims=True) + norm_eps)
    normed = rows_heads * inverse * gain_vector
    half_width = head_width // 2
    frequency = jnp.exp(
        jnp.arange(half_width, dtype=jnp.float32) * (-2.0 * math.log(rope_base) / head_width)
    )
    angles = token_pos.astype(jnp.float32)[:, None] * frequency[None, :]
    cosine_table = jnp.cos(angles)[:, None, :]
    sine_table = jnp.sin(angles)[:, None, :]
    first_half = normed[..., :half_width]
    second_half = normed[..., half_width:]
    return jnp.concatenate(
        [
            first_half * cosine_table - second_half * sine_table,
            second_half * cosine_table + first_half * sine_table,
        ],
        axis=-1,
    )


def shards(inputs, q_proj, k_proj, v_proj, d_attn, positions, windows, q_gain, k_gain, weight):
    tok_rows = inputs.shape[1]
    head_width = q_gain.shape[0]
    query_heads = q_proj.shape[2] // head_width
    key_heads = k_proj.shape[2] // head_width
    group_size = query_heads // key_heads
    token_pos = positions[0]
    window = windows[0]
    dp_count = lax.axis_size("dp")
    model_width = inputs.shape[2]
    input_parts = inputs[0].reshape(tok_rows, dp_count, model_width // dp_count).transpose(1, 0, 2)
    input_cols = lax.all_to_all(input_parts, "dp", split_axis=0, concat_axis=0, tiled=True)
    input_cols = input_cols.reshape(dp_count * tok_rows, model_width // dp_count)

    def query_side(projected_rows, gain_vector):
        return rotated_unit(projected_rows, gain_vector, token_pos, query_heads)

    def key_side(projected_rows, gain_vector):
        return rotated_unit(projected_rows, gain_vector, token_pos, key_heads)

    q_full, query_back = jax.vjp(query_side, q_proj[0].astype(jnp.float32), q_gain)
    k_full, key_back = jax.vjp(key_side, k_proj[0].astype(jnp.float32), k_gain)
    query_rotated = q_full.astype(jnp.bfloat16).reshape(tok_rows, key_heads, group_size, head_width)
    key_rotated = k_full.astype(jnp.bfloat16)
    v_own = v_proj[0].reshape(tok_rows, key_heads, head_width)
    reach_count = min(REACH, lax.axis_size("ctx") - 1)
    own_pair = jnp.stack([key_rotated, v_own])
    pair_blocks = [own_pair]
    for distance_steps in range(1, reach_count + 1):
        pair_blocks.append(from_behind(own_pair, "ctx", distance_steps))
    all_keys = jnp.stack([pair[0] for pair in pair_blocks])
    all_values = jnp.stack([pair[1] for pair in pair_blocks])
    block_ids = jnp.arange(reach_count + 1, dtype=jnp.int32)
    offsets = jnp.arange(tok_rows, dtype=jnp.int32)
    distance = block_ids[None, :, None] * tok_rows + offsets[:, None, None] - offsets[None, None, :]
    allowed = (distance >= 0) & (distance < window) & (distance <= token_pos[:, None, None])
    scores = (
        jnp.einsum("ahgd,bchd->hgabc", query_rotated, all_keys, preferred_element_type=jnp.float32)
        * score_scale
    )
    scores = jnp.where(allowed, scores, -jnp.inf)
    row_max = jnp.max(scores, axis=(3, 4), keepdims=True)
    exponent = jnp.exp(scores - row_max)
    probs = exponent / jnp.sum(exponent, axis=(3, 4), keepdims=True)
    head_gradient = d_attn[0].reshape(tok_rows, key_heads, group_size, head_width)
    dprobs = jnp.einsum(
        "ahgd,bchd->hgabc", head_gradient, all_values, preferred_element_type=jnp.float32
    )
    delta = jnp.sum(probs * dprobs, axis=(3, 4), keepdims=True)
    dscores = (probs * (dprobs - delta)).astype(jnp.bfloat16)
    probs_low = probs.astype(jnp.bfloat16)
    dq_rot = (
        jnp.einsum("hgabc,bchd->ahgd", dscores, all_keys, preferred_element_type=jnp.float32)
        * score_scale
    )
    dk_blocks = (
        jnp.einsum("hgabc,ahgd->bchd", dscores, query_rotated, preferred_element_type=jnp.float32)
        * score_scale
    )
    dv_blocks = jnp.einsum(
        "hgabc,ahgd->bchd", probs_low, head_gradient, preferred_element_type=jnp.float32
    )
    dq_proj, dq_gain = query_back(dq_rot.reshape(tok_rows, query_heads, head_width))
    query_all = lax.all_gather(dq_proj.astype(jnp.bfloat16), "dp", axis=0, tiled=True)
    pair_total = jnp.stack([dk_blocks[0], dv_blocks[0]])
    for distance_steps in range(1, reach_count + 1):
        far_pair = jnp.stack([dk_blocks[distance_steps], dv_blocks[distance_steps]])
        back_pair = from_behind(far_pair.astype(jnp.bfloat16), "ctx", -distance_steps)
        pair_total = pair_total + back_pair.astype(jnp.float32)
    dk_proj, dk_gain = key_back(pair_total[0])
    dq_gain_all, dk_gain_all = lax.psum((dq_gain, dk_gain), ("dp", "ctx"))
    dv_proj = pair_total[1].reshape(tok_rows, key_heads * head_width)
    d_keyval = jnp.concatenate([dk_proj, dv_proj], axis=-1).astype(jnp.bfloat16)
    keyval_all = lax.all_gather(d_keyval, "dp", axis=0, tiled=True)
    query_width = query_heads * head_width
    d_cols = jnp.einsum(
        "tp,dp->td", query_all, weight[:, :query_width], preferred_element_type=jnp.float32
    )
    d_cols = d_cols + jnp.einsum(
        "tp,dp->td", keyval_all, weight[:, query_width:], preferred_element_type=jnp.float32
    )
    d_parts = d_cols.astype(jnp.bfloat16).reshape(dp_count, tok_rows, model_width // dp_count)
    d_parts = lax.all_to_all(d_parts, "dp", split_axis=0, concat_axis=0, tiled=True)
    d_inputs = d_parts.transpose(1, 0, 2).reshape(1, tok_rows, model_width)
    halves = []
    for part in (query_all, keyval_all):
        term = jnp.einsum("tp,td->pd", part, input_cols, preferred_element_type=jnp.float32)
        halves.append(halved(term.astype(jnp.bfloat16), "ctx"))
    d_weight_t = owner_sum(halves, "ctx")
    return (d_inputs, d_weight_t, dq_gain_all, dk_gain_all)


def solution(mesh):
    placed = (
        P("dp", "ctx", None),
        P("dp", "ctx", None),
        P("dp", "ctx", None),
        P("dp", "ctx", None),
        P("dp", "ctx", None),
        P("dp", "ctx"),
        P("dp"),
        P(),
        P(),
        P("dp", None),
    )
    return jax.shard_map(
        shards,
        mesh=mesh,
        in_specs=placed,
        out_specs=(P("dp", "ctx", None), P("ctx", "dp"), P(), P()),
        check_vma=False,
    )
```

```python
import math

import jax
import jax.numpy as jnp
from jax import lax
from jax.sharding import PartitionSpec as P

REACH = 8


score_scale = 168.0 ** (-0.5)
rope_base = 10000.0
norm_eps = 1e-06


def from_behind(value, axis, steps):
    count = lax.axis_size(axis)
    initial, last = (max(0, -steps), min(count, count - steps))
    return lax.ppermute(value, axis, [(source, source + steps) for source in range(initial, last)])


def swapped(value, axis, bit):
    count = lax.axis_size(axis)
    return lax.ppermute(value, axis, [(source, source ^ bit) for source in range(count)])


def halved(term, axis):
    owners = lax.axis_size(axis) // 2
    side = (lax.axis_index(axis) & 1) == 1
    pieces = term.reshape(owners // 2, 2, term.shape[0] // owners, term.shape[1])
    kept = jnp.where(side, pieces[:, 1], pieces[:, 0])
    sent = jnp.where(side, pieces[:, 0], pieces[:, 1])
    got = swapped(sent, axis, 1)
    return kept.astype(jnp.float32) + got.astype(jnp.float32)


def owner_sum(halves, axis):
    count = lax.axis_size(axis)
    index = lax.axis_index(axis)
    low, high = halves
    bit = count // 2
    while bit >= 2:
        side = (index & bit) != 0
        kept = jnp.where(side, high, low)
        sent = jnp.where(side, low, high).astype(jnp.bfloat16)
        total = kept + swapped(sent, axis, bit).astype(jnp.float32)
        middle = total.shape[0] // 2
        low, high = total[:middle], total[middle:]
        bit //= 2
    return total.reshape(-1, total.shape[-1])


def rotated_unit(projected_rows, gain_vector, token_pos, head_count):
    head_width = gain_vector.shape[0]
    rows_heads = projected_rows.reshape(projected_rows.shape[0], head_count, head_width)
    inverse = lax.rsqrt(jnp.mean(rows_heads * rows_heads, axis=-1, keepdims=True) + norm_eps)
    normed = rows_heads * inverse * gain_vector
    half_width = head_width // 2
    frequency = jnp.exp(
        jnp.arange(half_width, dtype=jnp.float32) * (-2.0 * math.log(rope_base) / head_width)
    )
    angles = token_pos.astype(jnp.float32)[:, None] * frequency[None, :]
    cosine_table = jnp.cos(angles)[:, None, :]
    sine_table = jnp.sin(angles)[:, None, :]
    first_half = normed[..., :half_width]
    second_half = normed[..., half_width:]
    return jnp.concatenate(
        [
            first_half * cosine_table - second_half * sine_table,
            second_half * cosine_table + first_half * sine_table,
        ],
        axis=-1,
    )


def shards(inputs, q_proj, k_proj, v_proj, d_attn, positions, windows, q_gain, k_gain, weight):
    tok_rows = inputs.shape[1]
    head_width = q_gain.shape[0]
    query_heads = q_proj.shape[2] // head_width
    key_heads = k_proj.shape[2] // head_width
    group_size = query_heads // key_heads
    token_pos = positions[0]
    window = windows[0]
    dp_count = lax.axis_size("dp")
    model_width = inputs.shape[2]
    input_parts = inputs[0].reshape(tok_rows, dp_count, model_width // dp_count).transpose(1, 0, 2)
    input_cols = lax.all_to_all(input_parts, "dp", split_axis=0, concat_axis=0, tiled=True)
    input_cols = input_cols.reshape(dp_count * tok_rows, model_width // dp_count)

    def query_side(projected_rows, gain_vector):
        return rotated_unit(projected_rows, gain_vector, token_pos, query_heads)

    def key_side(projected_rows, gain_vector):
        return rotated_unit(projected_rows, gain_vector, token_pos, key_heads)

    q_full, query_back = jax.vjp(query_side, q_proj[0].astype(jnp.float32), q_gain)
    k_full, key_back = jax.vjp(key_side, k_proj[0].astype(jnp.float32), k_gain)
    query_rotated = q_full.astype(jnp.bfloat16).reshape(tok_rows, key_heads, group_size, head_width)
    key_rotated = k_full.astype(jnp.bfloat16)
    v_own = v_proj[0].reshape(tok_rows, key_heads, head_width)
    reach_count = min(REACH, lax.axis_size("ctx") - 1)
    own_pair = jnp.stack([key_rotated, v_own])
    pair_blocks = [own_pair]
    for distance_steps in range(1, reach_count + 1):
        pair_blocks.append(from_behind(own_pair, "ctx", distance_steps))
    all_keys = jnp.stack([pair[0] for pair in pair_blocks])
    all_values = jnp.stack([pair[1] for pair in pair_blocks])
    block_ids = jnp.arange(reach_count + 1, dtype=jnp.int32)
    offsets = jnp.arange(tok_rows, dtype=jnp.int32)
    distance = block_ids[None, :, None] * tok_rows + offsets[:, None, None] - offsets[None, None, :]
    allowed = (distance >= 0) & (distance < window) & (distance <= token_pos[:, None, None])
    scores = (
        jnp.einsum("ahgd,bchd->hgabc", query_rotated, all_keys, preferred_element_type=jnp.float32)
        * score_scale
    )
    scores = jnp.where(allowed, scores, -jnp.inf)
    row_max = jnp.max(scores, axis=(3, 4), keepdims=True)
    exponent = jnp.exp(scores - row_max)
    probs = exponent / jnp.sum(exponent, axis=(3, 4), keepdims=True)
    head_gradient = d_attn[0].reshape(tok_rows, key_heads, group_size, head_width)
    dprobs = jnp.einsum(
        "ahgd,bchd->hgabc", head_gradient, all_values, preferred_element_type=jnp.float32
    )
    delta = jnp.sum(probs * dprobs, axis=(3, 4), keepdims=True)
    dscores = (probs * (dprobs - delta)).astype(jnp.bfloat16)
    probs_low = probs.astype(jnp.bfloat16)
    dq_rot = (
        jnp.einsum("hgabc,bchd->ahgd", dscores, all_keys, preferred_element_type=jnp.float32)
        * score_scale
    )
    dk_blocks = (
        jnp.einsum("hgabc,ahgd->bchd", dscores, query_rotated, preferred_element_type=jnp.float32)
        * score_scale
    )
    dv_blocks = jnp.einsum(
        "hgabc,ahgd->bchd", probs_low, head_gradient, preferred_element_type=jnp.float32
    )
    dq_proj, dq_gain = query_back(dq_rot.reshape(tok_rows, query_heads, head_width))
    dq_proj, input_cols = lax.optimization_barrier((dq_proj, input_cols))
    query_all = lax.all_gather(dq_proj.astype(jnp.bfloat16), "dp", axis=0, tiled=True)
    pair_total = jnp.stack([dk_blocks[0], dv_blocks[0]])
    for distance_steps in range(1, reach_count + 1):
        far_pair = jnp.stack([dk_blocks[distance_steps], dv_blocks[distance_steps]])
        back_pair = from_behind(far_pair.astype(jnp.bfloat16), "ctx", -distance_steps)
        pair_total = pair_total + back_pair.astype(jnp.float32)
    dk_proj, dk_gain = key_back(pair_total[0])
    gain_terms = lax.all_gather(jnp.stack([dq_gain, dk_gain]), ("dp", "ctx"), axis=0)
    dq_gain_all, dk_gain_all = jnp.sum(gain_terms, axis=0)
    dv_proj = pair_total[1].reshape(tok_rows, key_heads * head_width)
    d_keyval = jnp.concatenate([dk_proj, dv_proj], axis=-1).astype(jnp.bfloat16)
    keyval_all = lax.all_gather(d_keyval, "dp", axis=0, tiled=True)
    query_width = query_heads * head_width
    d_cols = jnp.einsum(
        "tp,dp->td", query_all, weight[:, :query_width], preferred_element_type=jnp.float32
    )
    d_cols = d_cols + jnp.einsum(
        "tp,dp->td", keyval_all, weight[:, query_width:], preferred_element_type=jnp.float32
    )
    d_parts = d_cols.astype(jnp.bfloat16).reshape(dp_count, tok_rows, model_width // dp_count)
    d_parts = lax.all_to_all(d_parts, "dp", split_axis=0, concat_axis=0, tiled=True)
    d_inputs = d_parts.transpose(1, 0, 2).reshape(1, tok_rows, model_width)
    halves = []
    for part in (query_all, keyval_all):
        term = jnp.einsum("tp,td->pd", part, input_cols, preferred_element_type=jnp.float32)
        halves.append(halved(term.astype(jnp.bfloat16), "ctx"))
    d_weight_t = owner_sum(halves, "ctx")
    return (d_inputs, d_weight_t, dq_gain_all, dk_gain_all)


def solution(mesh):
    placed = (
        P("dp", "ctx", None),
        P("dp", "ctx", None),
        P("dp", "ctx", None),
        P("dp", "ctx", None),
        P("dp", "ctx", None),
        P("dp", "ctx"),
        P("dp"),
        P(),
        P(),
        P("dp", None),
    )
    return jax.shard_map(
        shards,
        mesh=mesh,
        in_specs=placed,
        out_specs=(P("dp", "ctx", None), P("ctx", "dp"), P(), P()),
        check_vma=False,
    )
```

```python
import math

import jax
import jax.numpy as jnp
from jax import lax
from jax.experimental import pallas as pl
from jax.experimental.pallas import tpu as pltpu
from jax.sharding import PartitionSpec as P

MESH = pl.DeviceIdType.MESH

REACH = 8


score_scale = 168.0 ** (-0.5)
rope_base = 10000.0
norm_eps = 1e-06


def from_behind(value, axis, steps):
    count = lax.axis_size(axis)
    initial, last = (max(0, -steps), min(count, count - steps))
    return lax.ppermute(value, axis, [(source, source + steps) for source in range(initial, last)])


def swapped(value, axis, bit):
    count = lax.axis_size(axis)
    return lax.ppermute(value, axis, [(source, source ^ bit) for source in range(count)])


def flipped(index, bits):
    bit = 1
    while bit <= bits:
        if bits & bit:
            index = index + bit - 2 * bit * (lax.rem(index // bit, 2))
        bit *= 2
    return index


def remote(source, target, send_sem, recv_sem, axis, index):
    return pltpu.make_async_remote_copy(
        src_ref=source,
        dst_ref=target,
        send_sem=send_sem,
        recv_sem=recv_sem,
        device_id={axis: index},
        device_id_type=MESH,
    )


def exchange_kernel(n_dp, n_ctx, reach, parts_ref, pair_ref, cols_ref, far_ref, own_sem, send_a, recv_a, send_b, recv_b):
    row = lax.axis_index("dp")
    col = lax.axis_index("ctx")
    barrier = pltpu.get_barrier_semaphore()
    for step in range(1, n_dp):
        pl.semaphore_signal(barrier, 1, device_id={"dp": lax.rem(row + step, n_dp)}, device_id_type=MESH)
    for step in range(1, n_ctx):
        pl.semaphore_signal(barrier, 1, device_id={"ctx": lax.rem(col + step, n_ctx)}, device_id_type=MESH)
    pl.semaphore_wait(barrier, n_dp + n_ctx - 2)
    for step in range(1, reach + 1):
        copy = remote(pair_ref, far_ref.at[step - 1], send_b.at[step], recv_b.at[step], "ctx", lax.rem(col + step, n_ctx))
        pl.when(col + step < n_ctx)(copy.start)
    own = pltpu.make_async_copy(parts_ref.at[row], cols_ref.at[row], own_sem)
    own.start()
    sends = []
    for step in range(1, n_dp):
        peer = lax.rem(row + step, n_dp)
        copy = remote(parts_ref.at[peer], cols_ref.at[row], send_a.at[step], recv_a.at[step], "dp", peer)
        copy.start()
        sends.append(copy)
    own.wait()
    for step in range(1, n_dp):
        source = lax.rem(row + n_dp - step, n_dp)
        remote(parts_ref.at[source], cols_ref.at[source], send_a.at[step], recv_a.at[step], "dp", source).wait_recv()
        sends[step - 1].wait_send()
    for step in range(1, reach + 1):
        copy = remote(pair_ref, far_ref.at[step - 1], send_b.at[step], recv_b.at[step], "ctx", lax.rem(col + step, n_ctx))
        pl.when(col + step < n_ctx)(copy.wait_send)
        pl.when(col >= step)(copy.wait_recv)


def exchanged(parts, pair, reach):
    n_dp, n_ctx = lax.axis_size("dp"), lax.axis_size("ctx")
    anywhere = pl.BlockSpec(memory_space=pl.ANY)
    dma = pltpu.SemaphoreType.DMA
    return pl.pallas_call(
        lambda *refs: exchange_kernel(n_dp, n_ctx, reach, *refs),
        out_shape=(
            jax.ShapeDtypeStruct(parts.shape, parts.dtype),
            jax.ShapeDtypeStruct((reach,) + pair.shape, pair.dtype),
        ),
        in_specs=[anywhere, anywhere],
        out_specs=(anywhere, anywhere),
        scratch_shapes=[dma, dma((n_dp,)), dma((n_dp,)), dma((reach + 1,)), dma((reach + 1,))],
        compiler_params=pltpu.CompilerParams(collective_id=1, has_side_effects=True),
        name="exchange",
    )(parts, pair)


def project_kernel(
    n_dp, n_ctx, d_ref, w_ref, cols_ref, back_ref, sum_ref,
    blocks, acc, outbox, terms, got, own_sem, send_g, recv_g, send_o, recv_o, send_w, recv_w,
):
    row = lax.axis_index("dp")
    col = lax.axis_index("ctx")
    line = n_dp // 2
    place = row // 2
    lane = lax.rem(row, 2)
    twin = 1 - 2 * lane
    width = w_ref.shape[1]
    bits = [1 << k for k in range(n_ctx.bit_length() - 1)]
    barrier = pltpu.get_barrier_semaphore()
    for step in range(1, n_dp):
        pl.semaphore_signal(barrier, 1, device_id={"dp": lax.rem(row + step, n_dp)}, device_id_type=MESH)
    for bit in bits:
        pl.semaphore_signal(barrier, 1, device_id={"ctx": flipped(col, bit)}, device_id_type=MESH)
    pl.semaphore_wait(barrier, n_dp - 1 + len(bits))

    def relay(block, way, target):
        return remote(blocks.at[block], blocks.at[block], send_g.at[way, block], recv_g.at[block], "dp", target)

    def arrived(block):
        relay(block, 0, lax.rem(row + 1, n_dp)).wait_recv()

    def back(block, target):
        return remote(outbox.at[block], back_ref.at[row], send_o.at[block], recv_o.at[row], "dp", target)

    def product(block):
        acc[...] = jnp.zeros_like(acc)
        depth = 1024

        @pl.loop(0, width // depth)
        def _(k):
            span = pl.ds(pl.multiple_of(k * depth, depth), depth)
            acc[...] += lax.dot_general(
                blocks[block, :, span], w_ref[:, span], (((1,), (1,)), ((), ())),
                preferred_element_type=jnp.float32,
            )

        outbox[block] = acc[...].astype(outbox.dtype)

    def answer(block):
        product(block)
        back(block, block).start()

    blocks[row] = d_ref[...]
    pl.when(place < line - 1)(lambda: relay(row, 0, row + 2).start())
    pl.when(place > 0)(lambda: relay(row, 1, row - 2).start())
    relay(row, 2, row + twin).start()
    product(row)
    own = pltpu.make_async_copy(outbox.at[row], back_ref.at[row], own_sem)
    own.start()

    @pl.loop(1, line + 1)
    def _(step):
        @pl.when(place >= step)
        def _():
            block = row - 2 * step
            arrived(block)
            pl.when(place < line - 1)(lambda: relay(block, 0, row + 2).start())
            relay(block, 2, row + twin).start()

        @pl.when(place + step < line)
        def _():
            block = row + 2 * step
            arrived(block)
            pl.when(place > 0)(lambda: relay(block, 1, row - 2).start())
            relay(block, 2, row + twin).start()

        pl.when(place >= step)(lambda: answer(row - 2 * step))
        pl.when(place + step < line)(lambda: answer(row + 2 * step))

        @pl.when(place >= step - 1)
        def _():
            block = row + twin - 2 * (step - 1)
            arrived(block)
            answer(block)

        @pl.when((step > 1) & (place + step - 1 < line))
        def _():
            block = row + twin + 2 * (step - 1)
            arrived(block)
            answer(block)

    tokens = n_dp * blocks.shape[1]
    rows = width // n_ctx
    tile = 256

    def fill(slot):
        start = flipped(col, slot) * rows

        @pl.loop(0, rows // tile)
        def _(k):
            span = pl.ds(pl.multiple_of(start + k * tile, tile), tile)
            left = blocks[:, :, span].reshape(tokens, tile)
            right = cols_ref[...].reshape(tokens, cols_ref.shape[2])
            term = lax.dot_general(
                left, right, (((0,), (0,)), ((), ())), preferred_element_type=jnp.float32
            )
            terms[slot, pl.ds(pl.multiple_of(k * tile, tile), tile), :] = term.astype(terms.dtype)

    def share(slot):
        bit = slot & -slot
        return remote(terms.at[slot], got.at[slot], send_w.at[slot], recv_w.at[slot], "ctx", flipped(col, bit))

    order = [slot for slot in range(n_ctx) if slot & 1] + [slot for slot in range(n_ctx) if not slot & 1][::-1]
    for slot in order:
        fill(slot)
        if slot & 1:
            share(slot).start()
    for bit in bits:
        for slot in reversed(range(0, n_ctx, 2 * bit)):
            share(slot + bit).wait_recv()
            if slot:
                total = terms[slot].astype(jnp.float32) + got[slot + bit].astype(jnp.float32)
                terms[slot] = total.astype(terms.dtype)
                if slot & (2 * bit):
                    share(slot).start()
            else:
                held = sum_ref[...] if bit > 1 else terms[0].astype(jnp.float32)
                sum_ref[...] = held + got[bit].astype(jnp.float32)
    for slot in range(1, n_ctx):
        share(slot).wait_send()
    own.wait()

    @pl.loop(1, n_dp)
    def _(step):
        source = lax.rem(row + step, n_dp)
        remote(outbox.at[source], back_ref.at[source], send_o.at[source], recv_o.at[source], "dp", source).wait_recv()
        back(source, source).wait_send()

    relay(row, 2, row + twin).wait_send()
    pl.when(place < line - 1)(lambda: relay(row, 0, row + 2).wait_send())
    pl.when(place > 0)(lambda: relay(row, 1, row - 2).wait_send())

    @pl.loop(1, line)
    def _(step):
        @pl.when(place >= step)
        def _():
            block = row - 2 * step
            pl.when(place < line - 1)(lambda: relay(block, 0, row + 2).wait_send())
            relay(block, 2, row + twin).wait_send()

        @pl.when(place + step < line)
        def _():
            block = row + 2 * step
            pl.when(place > 0)(lambda: relay(block, 1, row - 2).wait_send())
            relay(block, 2, row + twin).wait_send()


def projected(d_own, weight, cols):
    n_dp, n_ctx = lax.axis_size("dp"), lax.axis_size("ctx")
    toks, width = d_own.shape
    part = weight.shape[0]
    dma = pltpu.SemaphoreType.DMA
    vmem = pl.BlockSpec(memory_space=pltpu.VMEM)
    return pl.pallas_call(
        lambda *refs: project_kernel(n_dp, n_ctx, *refs),
        out_shape=(
            jax.ShapeDtypeStruct((n_dp, toks, part), jnp.bfloat16),
            jax.ShapeDtypeStruct((width // n_ctx, part), jnp.float32),
        ),
        in_specs=[vmem, vmem, vmem],
        out_specs=(pl.BlockSpec(memory_space=pl.ANY), vmem),
        scratch_shapes=[
            pltpu.VMEM((n_dp, toks, width), jnp.bfloat16),
            pltpu.VMEM((toks, part), jnp.float32),
            pltpu.VMEM((n_dp, toks, part), jnp.bfloat16),
            pltpu.VMEM((n_ctx, width // n_ctx, part), jnp.bfloat16),
            pltpu.VMEM((n_ctx, width // n_ctx, part), jnp.bfloat16),
            dma,
            dma((3, n_dp)),
            dma((n_dp,)),
            dma((n_dp,)),
            dma((n_dp,)),
            dma((n_ctx,)),
            dma((n_ctx,)),
        ],
        compiler_params=pltpu.CompilerParams(
            collective_id=2, has_side_effects=True, vmem_limit_bytes=56 * 1024 * 1024
        ),
        name="project",
    )(d_own, weight, cols)


def rotated_unit(projected_rows, gain_vector, token_pos, head_count):
    head_width = gain_vector.shape[0]
    rows_heads = projected_rows.reshape(projected_rows.shape[0], head_count, head_width)
    inverse = lax.rsqrt(jnp.mean(rows_heads * rows_heads, axis=-1, keepdims=True) + norm_eps)
    normed = rows_heads * inverse * gain_vector
    half_width = head_width // 2
    frequency = jnp.exp(
        jnp.arange(half_width, dtype=jnp.float32) * (-2.0 * math.log(rope_base) / head_width)
    )
    angles = token_pos.astype(jnp.float32)[:, None] * frequency[None, :]
    cosine_table = jnp.cos(angles)[:, None, :]
    sine_table = jnp.sin(angles)[:, None, :]
    first_half = normed[..., :half_width]
    second_half = normed[..., half_width:]
    return jnp.concatenate(
        [
            first_half * cosine_table - second_half * sine_table,
            second_half * cosine_table + first_half * sine_table,
        ],
        axis=-1,
    )


def shards(inputs, q_proj, k_proj, v_proj, d_attn, positions, windows, q_gain, k_gain, weight):
    tok_rows = inputs.shape[1]
    head_width = q_gain.shape[0]
    query_heads = q_proj.shape[2] // head_width
    key_heads = k_proj.shape[2] // head_width
    group_size = query_heads // key_heads
    token_pos = positions[0]
    window = windows[0]
    dp_count = lax.axis_size("dp")
    model_width = inputs.shape[2]
    input_parts = inputs[0].reshape(tok_rows, dp_count, model_width // dp_count).transpose(1, 0, 2)
    def query_side(projected_rows, gain_vector):
        return rotated_unit(projected_rows, gain_vector, token_pos, query_heads)

    def key_side(projected_rows, gain_vector):
        return rotated_unit(projected_rows, gain_vector, token_pos, key_heads)

    q_full, query_back = jax.vjp(query_side, q_proj[0].astype(jnp.float32), q_gain)
    k_full, key_back = jax.vjp(key_side, k_proj[0].astype(jnp.float32), k_gain)
    query_rotated = q_full.astype(jnp.bfloat16).reshape(tok_rows, key_heads, group_size, head_width)
    key_rotated = k_full.astype(jnp.bfloat16)
    v_own = v_proj[0].reshape(tok_rows, key_heads, head_width)
    reach_count = min(REACH, lax.axis_size("ctx") - 1)
    own_pair = jnp.stack([key_rotated, v_own])
    input_cols, far_pairs = exchanged(input_parts, own_pair, reach_count)
    known = jnp.arange(1, reach_count + 1) <= lax.axis_index("ctx")
    far_pairs = jnp.where(known[:, None, None, None, None], far_pairs, 0)
    all_keys = jnp.concatenate([key_rotated[None], far_pairs[:, 0]])
    all_values = jnp.concatenate([v_own[None], far_pairs[:, 1]])
    block_ids = jnp.arange(reach_count + 1, dtype=jnp.int32)
    offsets = jnp.arange(tok_rows, dtype=jnp.int32)
    distance = block_ids[None, :, None] * tok_rows + offsets[:, None, None] - offsets[None, None, :]
    allowed = (distance >= 0) & (distance < window) & (distance <= token_pos[:, None, None])
    scores = (
        jnp.einsum("ahgd,bchd->hgabc", query_rotated, all_keys, preferred_element_type=jnp.float32)
        * score_scale
    )
    scores = jnp.where(allowed, scores, -jnp.inf)
    row_max = jnp.max(scores, axis=(3, 4), keepdims=True)
    exponent = jnp.exp(scores - row_max)
    probs = exponent / jnp.sum(exponent, axis=(3, 4), keepdims=True)
    head_gradient = d_attn[0].reshape(tok_rows, key_heads, group_size, head_width)
    dprobs = jnp.einsum(
        "ahgd,bchd->hgabc", head_gradient, all_values, preferred_element_type=jnp.float32
    )
    delta = jnp.sum(probs * dprobs, axis=(3, 4), keepdims=True)
    dscores = (probs * (dprobs - delta)).astype(jnp.bfloat16)
    probs_low = probs.astype(jnp.bfloat16)
    dq_rot = (
        jnp.einsum("hgabc,bchd->ahgd", dscores, all_keys, preferred_element_type=jnp.float32)
        * score_scale
    )
    dk_blocks = (
        jnp.einsum("hgabc,ahgd->bchd", dscores, query_rotated, preferred_element_type=jnp.float32)
        * score_scale
    )
    dv_blocks = jnp.einsum(
        "hgabc,ahgd->bchd", probs_low, head_gradient, preferred_element_type=jnp.float32
    )
    dq_proj, dq_gain = query_back(dq_rot.reshape(tok_rows, query_heads, head_width))
    pair_total = jnp.stack([dk_blocks[0], dv_blocks[0]])
    for distance_steps in range(1, reach_count + 1):
        far_pair = jnp.stack([dk_blocks[distance_steps], dv_blocks[distance_steps]])
        back_pair = from_behind(far_pair.astype(jnp.bfloat16), "ctx", -distance_steps)
        pair_total = pair_total + back_pair.astype(jnp.float32)
    dk_proj, dk_gain = key_back(pair_total[0])
    dq_gain_all, dk_gain_all = lax.psum((dq_gain, dk_gain), ("dp", "ctx"))
    dv_proj = pair_total[1].reshape(tok_rows, key_heads * head_width)
    d_own = jnp.concatenate([dq_proj, dk_proj, dv_proj], axis=-1).astype(jnp.bfloat16)
    d_parts, d_weight_t = projected(d_own, weight, input_cols)
    d_inputs = d_parts.transpose(1, 0, 2).reshape(1, tok_rows, model_width)
    return (d_inputs, d_weight_t, dq_gain_all, dk_gain_all)


def solution(mesh):
    placed = (
        P("dp", "ctx", None),
        P("dp", "ctx", None),
        P("dp", "ctx", None),
        P("dp", "ctx", None),
        P("dp", "ctx", None),
        P("dp", "ctx"),
        P("dp"),
        P(),
        P(),
        P("dp", None),
    )
    return jax.shard_map(
        shards,
        mesh=mesh,
        in_specs=placed,
        out_specs=(P("dp", "ctx", None), P("ctx", "dp"), P(), P()),
        check_vma=False,
    )
```

```python
import math

import jax
import jax.numpy as jnp
from jax import lax
from jax.experimental import pallas as pl
from jax.experimental.pallas import tpu as pltpu
from jax.sharding import PartitionSpec as P

MESH = pl.DeviceIdType.MESH

REACH = 8


score_scale = 168.0 ** (-0.5)
rope_base = 10000.0
norm_eps = 1e-06


def from_behind(value, axis, steps):
    count = lax.axis_size(axis)
    initial, last = (max(0, -steps), min(count, count - steps))
    return lax.ppermute(value, axis, [(source, source + steps) for source in range(initial, last)])


def swapped(value, axis, bit):
    count = lax.axis_size(axis)
    return lax.ppermute(value, axis, [(source, source ^ bit) for source in range(count)])


def flipped(index, bits):
    bit = 1
    while bit <= bits:
        if bits & bit:
            index = index + bit - 2 * bit * (lax.rem(index // bit, 2))
        bit *= 2
    return index


def remote(source, target, send_sem, recv_sem, axis, index):
    return pltpu.make_async_remote_copy(
        src_ref=source,
        dst_ref=target,
        send_sem=send_sem,
        recv_sem=recv_sem,
        device_id={axis: index},
        device_id_type=MESH,
    )


def exchange_kernel(n_dp, n_ctx, reach, parts_ref, pair_ref, cols_ref, far_ref, own_sem, send_a, recv_a, send_b, recv_b):
    row = lax.axis_index("dp")
    col = lax.axis_index("ctx")
    barrier = pltpu.get_barrier_semaphore()
    for step in range(1, n_dp):
        pl.semaphore_signal(barrier, 1, device_id={"dp": lax.rem(row + step, n_dp)}, device_id_type=MESH)
    for step in range(1, n_ctx):
        pl.semaphore_signal(barrier, 1, device_id={"ctx": lax.rem(col + step, n_ctx)}, device_id_type=MESH)
    pl.semaphore_wait(barrier, n_dp + n_ctx - 2)
    for step in range(1, reach + 1):
        copy = remote(pair_ref, far_ref.at[step - 1], send_b.at[step], recv_b.at[step], "ctx", lax.rem(col + step, n_ctx))
        pl.when(col + step < n_ctx)(copy.start)
    own = pltpu.make_async_copy(parts_ref.at[row], cols_ref.at[row], own_sem)
    own.start()
    sends = []
    for step in range(1, n_dp):
        peer = lax.rem(row + step, n_dp)
        copy = remote(parts_ref.at[peer], cols_ref.at[row], send_a.at[step], recv_a.at[step], "dp", peer)
        copy.start()
        sends.append(copy)
    own.wait()
    for step in range(1, n_dp):
        source = lax.rem(row + n_dp - step, n_dp)
        remote(parts_ref.at[source], cols_ref.at[source], send_a.at[step], recv_a.at[step], "dp", source).wait_recv()
        sends[step - 1].wait_send()
    for step in range(1, reach + 1):
        copy = remote(pair_ref, far_ref.at[step - 1], send_b.at[step], recv_b.at[step], "ctx", lax.rem(col + step, n_ctx))
        pl.when(col + step < n_ctx)(copy.wait_send)
        pl.when(col >= step)(copy.wait_recv)


def exchanged(parts, pair, reach):
    n_dp, n_ctx = lax.axis_size("dp"), lax.axis_size("ctx")
    anywhere = pl.BlockSpec(memory_space=pl.ANY)
    dma = pltpu.SemaphoreType.DMA
    return pl.pallas_call(
        lambda *refs: exchange_kernel(n_dp, n_ctx, reach, *refs),
        out_shape=(
            jax.ShapeDtypeStruct(parts.shape, parts.dtype),
            jax.ShapeDtypeStruct((reach,) + pair.shape, pair.dtype),
        ),
        in_specs=[anywhere, anywhere],
        out_specs=(anywhere, anywhere),
        scratch_shapes=[dma, dma((n_dp,)), dma((n_dp,)), dma((reach + 1,)), dma((reach + 1,))],
        compiler_params=pltpu.CompilerParams(collective_id=1, has_side_effects=True),
        name="exchange",
    )(parts, pair)


def project_kernel(
    n_dp, n_ctx, d_ref, w_ref, cols_ref, gain_ref, back_ref, sum_ref, gain_out,
    blocks, acc, outbox, terms, got, gain_rows, gain_sent, gain_got,
    own_sem, send_g, recv_g, send_o, recv_o, send_w, recv_w, send_r, recv_r, send_c, recv_c,
):
    row = lax.axis_index("dp")
    col = lax.axis_index("ctx")
    line = n_dp // 2
    place = row // 2
    lane = lax.rem(row, 2)
    twin = 1 - 2 * lane
    width = w_ref.shape[1]
    bits = [1 << k for k in range(n_ctx.bit_length() - 1)]
    barrier = pltpu.get_barrier_semaphore()
    for step in range(1, n_dp):
        pl.semaphore_signal(barrier, 1, device_id={"dp": lax.rem(row + step, n_dp)}, device_id_type=MESH)
    for bit in bits:
        pl.semaphore_signal(barrier, 1, device_id={"ctx": flipped(col, bit)}, device_id_type=MESH)
    pl.semaphore_wait(barrier, n_dp - 1 + len(bits))

    def relay(block, way, target):
        return remote(blocks.at[block], blocks.at[block], send_g.at[way, block], recv_g.at[block], "dp", target)

    def arrived(block):
        relay(block, 0, lax.rem(row + 1, n_dp)).wait_recv()

    def back(block, target):
        return remote(outbox.at[block], back_ref.at[row], send_o.at[block], recv_o.at[row], "dp", target)

    def product(block):
        acc[...] = jnp.zeros_like(acc)
        depth = 1024

        @pl.loop(0, width // depth)
        def _(k):
            span = pl.ds(pl.multiple_of(k * depth, depth), depth)
            acc[...] += lax.dot_general(
                blocks[block, :, span], w_ref[:, span], (((1,), (1,)), ((), ())),
                preferred_element_type=jnp.float32,
            )

        outbox[block] = acc[...].astype(outbox.dtype)

    def answer(block):
        product(block)
        back(block, block).start()

    blocks[row] = d_ref[...]
    pl.when(place < line - 1)(lambda: relay(row, 0, row + 2).start())
    pl.when(place > 0)(lambda: relay(row, 1, row - 2).start())
    relay(row, 2, row + twin).start()

    def gain_to(peer):
        return remote(gain_ref, gain_rows.at[row], send_r.at[peer], recv_r.at[row], "dp", peer)

    gain_rows[row] = gain_ref[...]
    for step in range(1, n_dp):
        gain_to(lax.rem(row + step, n_dp)).start()
    product(row)
    own = pltpu.make_async_copy(outbox.at[row], back_ref.at[row], own_sem)
    own.start()

    @pl.loop(1, line + 1)
    def _(step):
        @pl.when(place >= step)
        def _():
            block = row - 2 * step
            arrived(block)
            pl.when(place < line - 1)(lambda: relay(block, 0, row + 2).start())
            relay(block, 2, row + twin).start()

        @pl.when(place + step < line)
        def _():
            block = row + 2 * step
            arrived(block)
            pl.when(place > 0)(lambda: relay(block, 1, row - 2).start())
            relay(block, 2, row + twin).start()

        pl.when(place >= step)(lambda: answer(row - 2 * step))
        pl.when(place + step < line)(lambda: answer(row + 2 * step))

        @pl.when(place >= step - 1)
        def _():
            block = row + twin - 2 * (step - 1)
            arrived(block)
            answer(block)

        @pl.when((step > 1) & (place + step - 1 < line))
        def _():
            block = row + twin + 2 * (step - 1)
            arrived(block)
            answer(block)

    tokens = n_dp * blocks.shape[1]
    rows = width // n_ctx
    tile = 256

    def fill(slot):
        start = flipped(col, slot) * rows

        @pl.loop(0, rows // tile)
        def _(k):
            span = pl.ds(pl.multiple_of(start + k * tile, tile), tile)
            left = blocks[:, :, span].reshape(tokens, tile)
            right = cols_ref[...].reshape(tokens, cols_ref.shape[2])
            term = lax.dot_general(
                left, right, (((0,), (0,)), ((), ())), preferred_element_type=jnp.float32
            )
            terms[slot, pl.ds(pl.multiple_of(k * tile, tile), tile), :] = term.astype(terms.dtype)

    def share(slot):
        bit = slot & -slot
        return remote(terms.at[slot], got.at[slot], send_w.at[slot], recv_w.at[slot], "ctx", flipped(col, bit))

    def merge(slot, bit):
        share(slot + bit).wait_recv()
        if slot:
            total = terms[slot].astype(jnp.float32) + got[slot + bit].astype(jnp.float32)
            terms[slot] = total.astype(terms.dtype)
            if slot & (2 * bit):
                share(slot).start()
        else:
            held = sum_ref[...] if bit > 1 else terms[0].astype(jnp.float32)
            sum_ref[...] = held + got[bit].astype(jnp.float32)

    for slot in reversed(range(0, n_ctx, 2)):
        fill(slot + 1)
        share(slot + 1).start()
        fill(slot)
        merge(slot, 1)

    for step in range(1, n_dp):
        peer = lax.rem(row + step, n_dp)
        remote(gain_ref, gain_rows.at[peer], send_r.at[peer], recv_r.at[peer], "dp", peer).wait_recv()
    gain_total = gain_rows[0]
    for peer in range(1, n_dp):
        gain_total = gain_total + gain_rows[peer]
    for level, bit in enumerate(bits):
        gain_sent[level] = gain_total
        copy = remote(
            gain_sent.at[level], gain_got.at[level], send_c.at[level], recv_c.at[level],
            "ctx", flipped(col, bit),
        )
        copy.start()
        copy.wait()
        gain_total = gain_total + gain_got[level]
    gain_out[...] = gain_total

    for bit in bits[1:]:
        for slot in reversed(range(0, n_ctx, 2 * bit)):
            merge(slot, bit)
    for step in range(1, n_dp):
        gain_to(lax.rem(row + step, n_dp)).wait_send()
    for slot in range(1, n_ctx):
        share(slot).wait_send()
    own.wait()

    @pl.loop(1, n_dp)
    def _(step):
        source = lax.rem(row + step, n_dp)
        remote(outbox.at[source], back_ref.at[source], send_o.at[source], recv_o.at[source], "dp", source).wait_recv()
        back(source, source).wait_send()

    relay(row, 2, row + twin).wait_send()
    pl.when(place < line - 1)(lambda: relay(row, 0, row + 2).wait_send())
    pl.when(place > 0)(lambda: relay(row, 1, row - 2).wait_send())

    @pl.loop(1, line)
    def _(step):
        @pl.when(place >= step)
        def _():
            block = row - 2 * step
            pl.when(place < line - 1)(lambda: relay(block, 0, row + 2).wait_send())
            relay(block, 2, row + twin).wait_send()

        @pl.when(place + step < line)
        def _():
            block = row + 2 * step
            pl.when(place > 0)(lambda: relay(block, 1, row - 2).wait_send())
            relay(block, 2, row + twin).wait_send()


def projected(d_own, weight, cols, gains):
    n_dp, n_ctx = lax.axis_size("dp"), lax.axis_size("ctx")
    toks, width = d_own.shape
    part = weight.shape[0]
    dma = pltpu.SemaphoreType.DMA
    levels = n_ctx.bit_length() - 1
    vmem = pl.BlockSpec(memory_space=pltpu.VMEM)
    return pl.pallas_call(
        lambda *refs: project_kernel(n_dp, n_ctx, *refs),
        out_shape=(
            jax.ShapeDtypeStruct((n_dp, toks, part), jnp.bfloat16),
            jax.ShapeDtypeStruct((width // n_ctx, part), jnp.float32),
            jax.ShapeDtypeStruct(gains.shape, jnp.float32),
        ),
        in_specs=[vmem, vmem, vmem, vmem],
        out_specs=(pl.BlockSpec(memory_space=pl.ANY), vmem, vmem),
        scratch_shapes=[
            pltpu.VMEM((n_dp, toks, width), jnp.bfloat16),
            pltpu.VMEM((toks, part), jnp.float32),
            pltpu.VMEM((n_dp, toks, part), jnp.bfloat16),
            pltpu.VMEM((n_ctx, width // n_ctx, part), jnp.bfloat16),
            pltpu.VMEM((n_ctx, width // n_ctx, part), jnp.bfloat16),
            pltpu.VMEM((n_dp,) + gains.shape, jnp.float32),
            pltpu.VMEM((levels,) + gains.shape, jnp.float32),
            pltpu.VMEM((levels,) + gains.shape, jnp.float32),
            dma,
            dma((3, n_dp)),
            dma((n_dp,)),
            dma((n_dp,)),
            dma((n_dp,)),
            dma((n_ctx,)),
            dma((n_ctx,)),
            dma((n_dp,)),
            dma((n_dp,)),
            dma((levels,)),
            dma((levels,)),
        ],
        compiler_params=pltpu.CompilerParams(
            collective_id=2, has_side_effects=True, vmem_limit_bytes=56 * 1024 * 1024
        ),
        name="project",
    )(d_own, weight, cols, gains)


def rotated_unit(projected_rows, gain_vector, token_pos, head_count):
    head_width = gain_vector.shape[0]
    rows_heads = projected_rows.reshape(projected_rows.shape[0], head_count, head_width)
    inverse = lax.rsqrt(jnp.mean(rows_heads * rows_heads, axis=-1, keepdims=True) + norm_eps)
    normed = rows_heads * inverse * gain_vector
    half_width = head_width // 2
    frequency = jnp.exp(
        jnp.arange(half_width, dtype=jnp.float32) * (-2.0 * math.log(rope_base) / head_width)
    )
    angles = token_pos.astype(jnp.float32)[:, None] * frequency[None, :]
    cosine_table = jnp.cos(angles)[:, None, :]
    sine_table = jnp.sin(angles)[:, None, :]
    first_half = normed[..., :half_width]
    second_half = normed[..., half_width:]
    return jnp.concatenate(
        [
            first_half * cosine_table - second_half * sine_table,
            second_half * cosine_table + first_half * sine_table,
        ],
        axis=-1,
    )


def shards(inputs, q_proj, k_proj, v_proj, d_attn, positions, windows, q_gain, k_gain, weight):
    tok_rows = inputs.shape[1]
    head_width = q_gain.shape[0]
    query_heads = q_proj.shape[2] // head_width
    key_heads = k_proj.shape[2] // head_width
    group_size = query_heads // key_heads
    token_pos = positions[0]
    window = windows[0]
    dp_count = lax.axis_size("dp")
    model_width = inputs.shape[2]
    input_parts = inputs[0].reshape(tok_rows, dp_count, model_width // dp_count).transpose(1, 0, 2)
    def query_side(projected_rows, gain_vector):
        return rotated_unit(projected_rows, gain_vector, token_pos, query_heads)

    def key_side(projected_rows, gain_vector):
        return rotated_unit(projected_rows, gain_vector, token_pos, key_heads)

    q_full, query_back = jax.vjp(query_side, q_proj[0].astype(jnp.float32), q_gain)
    k_full, key_back = jax.vjp(key_side, k_proj[0].astype(jnp.float32), k_gain)
    query_rotated = q_full.astype(jnp.bfloat16).reshape(tok_rows, key_heads, group_size, head_width)
    key_rotated = k_full.astype(jnp.bfloat16)
    v_own = v_proj[0].reshape(tok_rows, key_heads, head_width)
    reach_count = min(REACH, lax.axis_size("ctx") - 1)
    own_pair = jnp.stack([key_rotated, v_own])
    input_cols, far_pairs = exchanged(input_parts, own_pair, reach_count)
    known = jnp.arange(1, reach_count + 1) <= lax.axis_index("ctx")
    far_pairs = jnp.where(known[:, None, None, None, None], far_pairs, 0)
    all_keys = jnp.concatenate([key_rotated[None], far_pairs[:, 0]])
    all_values = jnp.concatenate([v_own[None], far_pairs[:, 1]])
    block_ids = jnp.arange(reach_count + 1, dtype=jnp.int32)
    offsets = jnp.arange(tok_rows, dtype=jnp.int32)
    distance = block_ids[None, :, None] * tok_rows + offsets[:, None, None] - offsets[None, None, :]
    allowed = (distance >= 0) & (distance < window) & (distance <= token_pos[:, None, None])
    scores = (
        jnp.einsum("ahgd,bchd->hgabc", query_rotated, all_keys, preferred_element_type=jnp.float32)
        * score_scale
    )
    scores = jnp.where(allowed, scores, -jnp.inf)
    row_max = jnp.max(scores, axis=(3, 4), keepdims=True)
    exponent = jnp.exp(scores - row_max)
    probs = exponent / jnp.sum(exponent, axis=(3, 4), keepdims=True)
    head_gradient = d_attn[0].reshape(tok_rows, key_heads, group_size, head_width)
    dprobs = jnp.einsum(
        "ahgd,bchd->hgabc", head_gradient, all_values, preferred_element_type=jnp.float32
    )
    delta = jnp.sum(probs * dprobs, axis=(3, 4), keepdims=True)
    dscores = (probs * (dprobs - delta)).astype(jnp.bfloat16)
    probs_low = probs.astype(jnp.bfloat16)
    dq_rot = (
        jnp.einsum("hgabc,bchd->ahgd", dscores, all_keys, preferred_element_type=jnp.float32)
        * score_scale
    )
    dk_blocks = (
        jnp.einsum("hgabc,ahgd->bchd", dscores, query_rotated, preferred_element_type=jnp.float32)
        * score_scale
    )
    dv_blocks = jnp.einsum(
        "hgabc,ahgd->bchd", probs_low, head_gradient, preferred_element_type=jnp.float32
    )
    dq_proj, dq_gain = query_back(dq_rot.reshape(tok_rows, query_heads, head_width))
    pair_total = jnp.stack([dk_blocks[0], dv_blocks[0]])
    for distance_steps in range(1, reach_count + 1):
        far_pair = jnp.stack([dk_blocks[distance_steps], dv_blocks[distance_steps]])
        back_pair = from_behind(far_pair.astype(jnp.bfloat16), "ctx", -distance_steps)
        pair_total = pair_total + back_pair.astype(jnp.float32)
    dk_proj, dk_gain = key_back(pair_total[0])
    dv_proj = pair_total[1].reshape(tok_rows, key_heads * head_width)
    d_own = jnp.concatenate([dq_proj, dk_proj, dv_proj], axis=-1).astype(jnp.bfloat16)
    gains = jnp.pad(jnp.stack([dq_gain, dk_gain]), ((0, 6), (0, 0)))
    d_parts, d_weight_t, gain_sums = projected(d_own, weight, input_cols, gains)
    dq_gain_all, dk_gain_all = gain_sums[0], gain_sums[1]
    d_inputs = d_parts.transpose(1, 0, 2).reshape(1, tok_rows, model_width)
    return (d_inputs, d_weight_t, dq_gain_all, dk_gain_all)


def solution(mesh):
    placed = (
        P("dp", "ctx", None),
        P("dp", "ctx", None),
        P("dp", "ctx", None),
        P("dp", "ctx", None),
        P("dp", "ctx", None),
        P("dp", "ctx"),
        P("dp"),
        P(),
        P(),
        P("dp", None),
    )
    return jax.shard_map(
        shards,
        mesh=mesh,
        in_specs=placed,
        out_specs=(P("dp", "ctx", None), P("ctx", "dp"), P(), P()),
        check_vma=False,
    )
```

```python
import math

import jax
import jax.numpy as jnp
from jax import lax
from jax.experimental import pallas as pl
from jax.experimental.pallas import tpu as pltpu
from jax.sharding import PartitionSpec as P

MESH = pl.DeviceIdType.MESH

REACH = 8


score_scale = 168.0 ** (-0.5)
rope_base = 10000.0
norm_eps = 1e-06


def from_behind(value, axis, steps):
    count = lax.axis_size(axis)
    initial, last = (max(0, -steps), min(count, count - steps))
    return lax.ppermute(value, axis, [(source, source + steps) for source in range(initial, last)])


def swapped(value, axis, bit):
    count = lax.axis_size(axis)
    return lax.ppermute(value, axis, [(source, source ^ bit) for source in range(count)])


def flipped(index, bits):
    bit = 1
    while bit <= bits:
        if bits & bit:
            index = index + bit - 2 * bit * (lax.rem(index // bit, 2))
        bit *= 2
    return index


def remote(source, target, send_sem, recv_sem, axis, index):
    return pltpu.make_async_remote_copy(
        src_ref=source,
        dst_ref=target,
        send_sem=send_sem,
        recv_sem=recv_sem,
        device_id={axis: index},
        device_id_type=MESH,
    )


def exchange_kernel(n_dp, n_ctx, reach, parts_ref, pair_ref, cols_ref, far_ref, own_sem, send_a, recv_a, send_b, recv_b):
    row = lax.axis_index("dp")
    col = lax.axis_index("ctx")
    barrier = pltpu.get_barrier_semaphore()
    for step in range(1, n_dp):
        pl.semaphore_signal(barrier, 1, device_id={"dp": lax.rem(row + step, n_dp)}, device_id_type=MESH)
    for step in range(1, n_ctx):
        pl.semaphore_signal(barrier, 1, device_id={"ctx": lax.rem(col + step, n_ctx)}, device_id_type=MESH)
    pl.semaphore_wait(barrier, n_dp + n_ctx - 2)
    for step in range(1, reach + 1):
        copy = remote(pair_ref, far_ref.at[step - 1], send_b.at[step], recv_b.at[step], "ctx", lax.rem(col + step, n_ctx))
        pl.when(col + step < n_ctx)(copy.start)
    own = pltpu.make_async_copy(parts_ref.at[row], cols_ref.at[row], own_sem)
    own.start()
    sends = []
    for step in range(1, n_dp):
        peer = lax.rem(row + step, n_dp)
        copy = remote(parts_ref.at[peer], cols_ref.at[row], send_a.at[step], recv_a.at[step], "dp", peer)
        copy.start()
        sends.append(copy)
    own.wait()
    for step in range(1, n_dp):
        source = lax.rem(row + n_dp - step, n_dp)
        remote(parts_ref.at[source], cols_ref.at[source], send_a.at[step], recv_a.at[step], "dp", source).wait_recv()
        sends[step - 1].wait_send()
    for step in range(1, reach + 1):
        copy = remote(pair_ref, far_ref.at[step - 1], send_b.at[step], recv_b.at[step], "ctx", lax.rem(col + step, n_ctx))
        pl.when(col + step < n_ctx)(copy.wait_send)
        pl.when(col >= step)(copy.wait_recv)


def exchanged(parts, pair, reach):
    n_dp, n_ctx = lax.axis_size("dp"), lax.axis_size("ctx")
    anywhere = pl.BlockSpec(memory_space=pl.ANY)
    dma = pltpu.SemaphoreType.DMA
    return pl.pallas_call(
        lambda *refs: exchange_kernel(n_dp, n_ctx, reach, *refs),
        out_shape=(
            jax.ShapeDtypeStruct(parts.shape, parts.dtype),
            jax.ShapeDtypeStruct((reach,) + pair.shape, pair.dtype),
        ),
        in_specs=[anywhere, anywhere],
        out_specs=(anywhere, anywhere),
        scratch_shapes=[dma, dma((n_dp,)), dma((n_dp,)), dma((reach + 1,)), dma((reach + 1,))],
        compiler_params=pltpu.CompilerParams(collective_id=1, has_side_effects=True),
        name="exchange",
    )(parts, pair)


def project_kernel(
    n_dp, n_ctx, d_ref, w_ref, cols_ref, gain_ref, back_ref, sum_ref, gain_out,
    blocks, acc, outbox, terms, got, gain_rows, gain_sent, gain_got,
    own_sem, send_g, recv_g, send_o, recv_o, send_w, recv_w, send_r, recv_r, send_c, recv_c,
):
    row = lax.axis_index("dp")
    col = lax.axis_index("ctx")
    line = n_dp // 2
    place = row // 2
    lane = lax.rem(row, 2)
    twin = 1 - 2 * lane
    width = w_ref.shape[1]
    bits = [1 << k for k in range(n_ctx.bit_length() - 1)]
    barrier = pltpu.get_barrier_semaphore()
    for step in range(1, n_dp):
        pl.semaphore_signal(barrier, 1, device_id={"dp": lax.rem(row + step, n_dp)}, device_id_type=MESH)
    for bit in bits:
        pl.semaphore_signal(barrier, 1, device_id={"ctx": flipped(col, bit)}, device_id_type=MESH)
    pl.semaphore_wait(barrier, n_dp - 1 + len(bits))

    def relay(block, way, target):
        return remote(blocks.at[block], blocks.at[block], send_g.at[way, block], recv_g.at[block], "dp", target)

    def arrived(block):
        relay(block, 0, lax.rem(row + 1, n_dp)).wait_recv()

    def back(block, target):
        return remote(outbox.at[block], back_ref.at[row], send_o.at[block], recv_o.at[row], "dp", target)

    def product(block):
        acc[...] = jnp.zeros_like(acc)
        depth = 2048

        @pl.loop(0, width // depth)
        def _(k):
            span = pl.ds(pl.multiple_of(k * depth, depth), depth)
            acc[...] += lax.dot_general(
                blocks[block, :, span], w_ref[:, span], (((1,), (1,)), ((), ())),
                preferred_element_type=jnp.float32,
            )

        outbox[block] = acc[...].astype(outbox.dtype)

    def answer(block):
        product(block)
        back(block, block).start()

    blocks[row] = d_ref[...]
    pl.when(place < line - 1)(lambda: relay(row, 0, row + 2).start())
    pl.when(place > 0)(lambda: relay(row, 1, row - 2).start())
    relay(row, 2, row + twin).start()

    def gain_to(peer):
        return remote(gain_ref, gain_rows.at[row], send_r.at[peer], recv_r.at[row], "dp", peer)

    gain_rows[row] = gain_ref[...]
    for step in range(1, n_dp):
        gain_to(lax.rem(row + step, n_dp)).start()
    product(row)
    own = pltpu.make_async_copy(outbox.at[row], back_ref.at[row], own_sem)
    own.start()

    @pl.loop(1, line + 1)
    def _(step):
        @pl.when(place >= step)
        def _():
            block = row - 2 * step
            arrived(block)
            pl.when(place < line - 1)(lambda: relay(block, 0, row + 2).start())
            relay(block, 2, row + twin).start()

        @pl.when(place + step < line)
        def _():
            block = row + 2 * step
            arrived(block)
            pl.when(place > 0)(lambda: relay(block, 1, row - 2).start())
            relay(block, 2, row + twin).start()

        pl.when(place >= step)(lambda: answer(row - 2 * step))
        pl.when(place + step < line)(lambda: answer(row + 2 * step))

        @pl.when(place >= step - 1)
        def _():
            block = row + twin - 2 * (step - 1)
            arrived(block)
            answer(block)

        @pl.when((step > 1) & (place + step - 1 < line))
        def _():
            block = row + twin + 2 * (step - 1)
            arrived(block)
            answer(block)

    tokens = n_dp * blocks.shape[1]
    rows = width // n_ctx
    tile = min(512, rows)

    def fill(slot):
        start = flipped(col, slot) * rows

        @pl.loop(0, rows // tile)
        def _(k):
            span = pl.ds(pl.multiple_of(start + k * tile, tile), tile)
            left = blocks[:, :, span].reshape(tokens, tile)
            right = cols_ref[...].reshape(tokens, cols_ref.shape[2])
            term = lax.dot_general(
                left, right, (((0,), (0,)), ((), ())), preferred_element_type=jnp.float32
            )
            terms[slot, pl.ds(pl.multiple_of(k * tile, tile), tile), :] = term.astype(terms.dtype)

    def share(slot):
        bit = slot & -slot
        return remote(terms.at[slot], got.at[slot], send_w.at[slot], recv_w.at[slot], "ctx", flipped(col, bit))

    def merge(slot, bit):
        share(slot + bit).wait_recv()
        if slot:
            total = terms[slot].astype(jnp.float32) + got[slot + bit].astype(jnp.float32)
            terms[slot] = total.astype(terms.dtype)
            if slot & (2 * bit):
                share(slot).start()
        else:
            held = sum_ref[...] if bit > 1 else terms[0].astype(jnp.float32)
            sum_ref[...] = held + got[bit].astype(jnp.float32)

    for slot in reversed(range(0, n_ctx, 2)):
        fill(slot + 1)
        share(slot + 1).start()
        fill(slot)
        merge(slot, 1)

    for step in range(1, n_dp):
        peer = lax.rem(row + step, n_dp)
        remote(gain_ref, gain_rows.at[peer], send_r.at[peer], recv_r.at[peer], "dp", peer).wait_recv()
    gain_total = gain_rows[0]
    for peer in range(1, n_dp):
        gain_total = gain_total + gain_rows[peer]
    for level, bit in enumerate(bits):
        gain_sent[level] = gain_total
        copy = remote(
            gain_sent.at[level], gain_got.at[level], send_c.at[level], recv_c.at[level],
            "ctx", flipped(col, bit),
        )
        copy.start()
        copy.wait()
        gain_total = gain_total + gain_got[level]
    gain_out[...] = gain_total

    for bit in bits[1:]:
        for slot in reversed(range(0, n_ctx, 2 * bit)):
            merge(slot, bit)
    for step in range(1, n_dp):
        gain_to(lax.rem(row + step, n_dp)).wait_send()
    for slot in range(1, n_ctx):
        share(slot).wait_send()
    own.wait()

    @pl.loop(1, n_dp)
    def _(step):
        source = lax.rem(row + step, n_dp)
        remote(outbox.at[source], back_ref.at[source], send_o.at[source], recv_o.at[source], "dp", source).wait_recv()
        back(source, source).wait_send()

    relay(row, 2, row + twin).wait_send()
    pl.when(place < line - 1)(lambda: relay(row, 0, row + 2).wait_send())
    pl.when(place > 0)(lambda: relay(row, 1, row - 2).wait_send())

    @pl.loop(1, line)
    def _(step):
        @pl.when(place >= step)
        def _():
            block = row - 2 * step
            pl.when(place < line - 1)(lambda: relay(block, 0, row + 2).wait_send())
            relay(block, 2, row + twin).wait_send()

        @pl.when(place + step < line)
        def _():
            block = row + 2 * step
            pl.when(place > 0)(lambda: relay(block, 1, row - 2).wait_send())
            relay(block, 2, row + twin).wait_send()


def projected(d_own, weight, cols, gains):
    n_dp, n_ctx = lax.axis_size("dp"), lax.axis_size("ctx")
    toks, width = d_own.shape
    part = weight.shape[0]
    dma = pltpu.SemaphoreType.DMA
    levels = n_ctx.bit_length() - 1
    vmem = pl.BlockSpec(memory_space=pltpu.VMEM)
    return pl.pallas_call(
        lambda *refs: project_kernel(n_dp, n_ctx, *refs),
        out_shape=(
            jax.ShapeDtypeStruct((n_dp, toks, part), jnp.bfloat16),
            jax.ShapeDtypeStruct((width // n_ctx, part), jnp.float32),
            jax.ShapeDtypeStruct(gains.shape, jnp.float32),
        ),
        in_specs=[vmem, vmem, vmem, vmem],
        out_specs=(pl.BlockSpec(memory_space=pl.ANY), vmem, vmem),
        scratch_shapes=[
            pltpu.VMEM((n_dp, toks, width), jnp.bfloat16),
            pltpu.VMEM((toks, part), jnp.float32),
            pltpu.VMEM((n_dp, toks, part), jnp.bfloat16),
            pltpu.VMEM((n_ctx, width // n_ctx, part), jnp.bfloat16),
            pltpu.VMEM((n_ctx, width // n_ctx, part), jnp.bfloat16),
            pltpu.VMEM((n_dp,) + gains.shape, jnp.float32),
            pltpu.VMEM((levels,) + gains.shape, jnp.float32),
            pltpu.VMEM((levels,) + gains.shape, jnp.float32),
            dma,
            dma((3, n_dp)),
            dma((n_dp,)),
            dma((n_dp,)),
            dma((n_dp,)),
            dma((n_ctx,)),
            dma((n_ctx,)),
            dma((n_dp,)),
            dma((n_dp,)),
            dma((levels,)),
            dma((levels,)),
        ],
        compiler_params=pltpu.CompilerParams(
            collective_id=2, has_side_effects=True, vmem_limit_bytes=56 * 1024 * 1024
        ),
        name="project",
    )(d_own, weight, cols, gains)


def rotated_unit(projected_rows, gain_vector, token_pos, head_count):
    head_width = gain_vector.shape[0]
    rows_heads = projected_rows.reshape(projected_rows.shape[0], head_count, head_width)
    inverse = lax.rsqrt(jnp.mean(rows_heads * rows_heads, axis=-1, keepdims=True) + norm_eps)
    normed = rows_heads * inverse * gain_vector
    half_width = head_width // 2
    frequency = jnp.exp(
        jnp.arange(half_width, dtype=jnp.float32) * (-2.0 * math.log(rope_base) / head_width)
    )
    angles = token_pos.astype(jnp.float32)[:, None] * frequency[None, :]
    cosine_table = jnp.cos(angles)[:, None, :]
    sine_table = jnp.sin(angles)[:, None, :]
    first_half = normed[..., :half_width]
    second_half = normed[..., half_width:]
    return jnp.concatenate(
        [
            first_half * cosine_table - second_half * sine_table,
            second_half * cosine_table + first_half * sine_table,
        ],
        axis=-1,
    )


def shards(inputs, q_proj, k_proj, v_proj, d_attn, positions, windows, q_gain, k_gain, weight):
    tok_rows = inputs.shape[1]
    head_width = q_gain.shape[0]
    query_heads = q_proj.shape[2] // head_width
    key_heads = k_proj.shape[2] // head_width
    group_size = query_heads // key_heads
    token_pos = positions[0]
    window = windows[0]
    dp_count = lax.axis_size("dp")
    model_width = inputs.shape[2]
    input_parts = inputs[0].reshape(tok_rows, dp_count, model_width // dp_count).transpose(1, 0, 2)
    def query_side(projected_rows, gain_vector):
        return rotated_unit(projected_rows, gain_vector, token_pos, query_heads)

    def key_side(projected_rows, gain_vector):
        return rotated_unit(projected_rows, gain_vector, token_pos, key_heads)

    q_full, query_back = jax.vjp(query_side, q_proj[0].astype(jnp.float32), q_gain)
    k_full, key_back = jax.vjp(key_side, k_proj[0].astype(jnp.float32), k_gain)
    query_rotated = q_full.astype(jnp.bfloat16).reshape(tok_rows, key_heads, group_size, head_width)
    key_rotated = k_full.astype(jnp.bfloat16)
    v_own = v_proj[0].reshape(tok_rows, key_heads, head_width)
    reach_count = min(REACH, lax.axis_size("ctx") - 1)
    own_pair = jnp.stack([key_rotated, v_own])
    input_cols, far_pairs = exchanged(input_parts, own_pair, reach_count)
    known = jnp.arange(1, reach_count + 1) <= lax.axis_index("ctx")
    far_pairs = jnp.where(known[:, None, None, None, None], far_pairs, 0)
    all_keys = jnp.concatenate([key_rotated[None], far_pairs[:, 0]])
    all_values = jnp.concatenate([v_own[None], far_pairs[:, 1]])
    block_ids = jnp.arange(reach_count + 1, dtype=jnp.int32)
    offsets = jnp.arange(tok_rows, dtype=jnp.int32)
    distance = block_ids[None, :, None] * tok_rows + offsets[:, None, None] - offsets[None, None, :]
    allowed = (distance >= 0) & (distance < window) & (distance <= token_pos[:, None, None])
    scores = (
        jnp.einsum("ahgd,bchd->hgabc", query_rotated, all_keys, preferred_element_type=jnp.float32)
        * score_scale
    )
    scores = jnp.where(allowed, scores, -jnp.inf)
    row_max = jnp.max(scores, axis=(3, 4), keepdims=True)
    exponent = jnp.exp(scores - row_max)
    probs = exponent / jnp.sum(exponent, axis=(3, 4), keepdims=True)
    head_gradient = d_attn[0].reshape(tok_rows, key_heads, group_size, head_width)
    dprobs = jnp.einsum(
        "ahgd,bchd->hgabc", head_gradient, all_values, preferred_element_type=jnp.float32
    )
    delta = jnp.sum(probs * dprobs, axis=(3, 4), keepdims=True)
    dscores = (probs * (dprobs - delta)).astype(jnp.bfloat16)
    probs_low = probs.astype(jnp.bfloat16)
    dq_rot = (
        jnp.einsum("hgabc,bchd->ahgd", dscores, all_keys, preferred_element_type=jnp.float32)
        * score_scale
    )
    dk_blocks = (
        jnp.einsum("hgabc,ahgd->bchd", dscores, query_rotated, preferred_element_type=jnp.float32)
        * score_scale
    )
    dv_blocks = jnp.einsum(
        "hgabc,ahgd->bchd", probs_low, head_gradient, preferred_element_type=jnp.float32
    )
    dq_proj, dq_gain = query_back(dq_rot.reshape(tok_rows, query_heads, head_width))
    pair_total = jnp.stack([dk_blocks[0], dv_blocks[0]])
    for distance_steps in range(1, reach_count + 1):
        far_pair = jnp.stack([dk_blocks[distance_steps], dv_blocks[distance_steps]])
        back_pair = from_behind(far_pair.astype(jnp.bfloat16), "ctx", -distance_steps)
        pair_total = pair_total + back_pair.astype(jnp.float32)
    dk_proj, dk_gain = key_back(pair_total[0])
    dv_proj = pair_total[1].reshape(tok_rows, key_heads * head_width)
    d_own = jnp.concatenate([dq_proj, dk_proj, dv_proj], axis=-1).astype(jnp.bfloat16)
    gains = jnp.pad(jnp.stack([dq_gain, dk_gain]), ((0, 6), (0, 0)))
    d_parts, d_weight_t, gain_sums = projected(d_own, weight, input_cols, gains)
    dq_gain_all, dk_gain_all = gain_sums[0], gain_sums[1]
    d_inputs = d_parts.transpose(1, 0, 2).reshape(1, tok_rows, model_width)
    return (d_inputs, d_weight_t, dq_gain_all, dk_gain_all)


def solution(mesh):
    placed = (
        P("dp", "ctx", None),
        P("dp", "ctx", None),
        P("dp", "ctx", None),
        P("dp", "ctx", None),
        P("dp", "ctx", None),
        P("dp", "ctx"),
        P("dp"),
        P(),
        P(),
        P("dp", None),
    )
    return jax.shard_map(
        shards,
        mesh=mesh,
        in_specs=placed,
        out_specs=(P("dp", "ctx", None), P("ctx", "dp"), P(), P()),
        check_vma=False,
    )
```
